512 devices in a mesh: section: 8 (over x, core), expert: 64 (over y, z).
Axes of the slice: x: 4, y: 4, z: 16, core: 2. Of those that a mesh axis runs over, the one named last changes fastest.
Arguments:
- entering: bfloat16 [8, 2048, 3584], P('section', 'expert'), may hold values from -6 to 6
- saved: bfloat16 [8, 64, 384, 384], P('section', 'expert'), may hold values from -6 to 6
- routes: int32 [2, 8, 2048, 1], P(None, 'section', 'expert'), may hold values from 0 to 7; in each aligned block of 32 rows (0 to 31, 32 to 63, ..., all dimensions but the last counted through in order) at most 6 rows name the same one
- gates: float32 [2, 8, 2048, 1], P(None, 'section', 'expert'), may hold values from 0.1 to 1
- w_in: bfloat16 [8, 64, 3584, 384], P('section', 'expert'), may hold values from -0.09375 to 0.09375
- w_out: bfloat16 [8, 64, 192, 3584], P('section', 'expert'), may hold values from -0.15625 to 0.15625
Outputs:
- results: bfloat16 [2, 8, 2048, 3584], P(None, 'section', 'expert')
The draws below stay inside these ranges and needn't reach their ends.
Inputs may be any that keep to these rules, and one draw needn't show every extreme that they name: `routes`: each row names one expert; in the rows of one device for one tick and layer no expert is named more than 6 times.
All inputs are finite; a program needn't handle non-finite values.
Results may differ from the reference program's by a relative error of at most 0.015.
Values may be sent and summed in bfloat16 or wider, within the bound.
No kernel may reach another device: no remote copies, remote signals or barrier semaphores. Data moves between devices by JAX's collectives and lax.ppermute only.
A program may use at most 64 MiB of HBM per device.

```python
import math
import jax
import jax.numpy as jnp
import numpy as np
from jax import lax

D = 3584
F = 1536
SHARDS = 8
TOP = 1
TOK_DEV = 32
SECTIONS = 8
EXPERTS = 8
HDEV = 192
TOKENS = 2048
CAP = 6
N_EXPERT = 64


def block_levels(key, extent, pieces, smallest, top_value):
    gain, own = 1.0, jax.random.fold_in(key, 6)
    for position, parts in pieces:
        steps = jnp.exp(jax.random.uniform(jax.random.fold_in(own, position), (parts,), jnp.float32, smallest / len(pieces), top_value / len(pieces)))
        gain = gain * jnp.repeat(steps, extent[position] // parts).reshape([-1 if axis == position else 1 for axis in range(len(extent))])
    return gain


def assign_block(rng, own, number, rows, count, top, bound, slope):
    ranking = jax.random.permutation(rng, count)
    crowded, ordinary = load_shares(count, rows * top, bound, slope, True), load_shares(count, rows * top, bound, slope, False)
    places = jnp.arange(count)

    def named(lengths, offset_by):
        used = int((lengths > 0).sum())
        fixed = max(1, used // 4)
        moved = fixed + (places - fixed + offset_by * (used - fixed)) % max(1, count - fixed)
        return jnp.zeros((count,), jnp.int32).at[ranking[jnp.where(places < fixed, places, moved)]].set(jnp.asarray(lengths, jnp.int32))

    lengths = jnp.where(number % 4 == 0, named(crowded, number // 4), named(ordinary, number - number // 4 - 1))
    mixed = jax.random.permutation(jax.random.fold_in(own, 3), count)
    donor, sink = mixed[0:count // 2 * 2:2], mixed[1:count // 2 * 2:2]
    slack = jnp.minimum(lengths[donor] - 1, bound - lengths[sink]) // 2
    slack = jnp.where((donor == ranking[0]) | (sink == ranking[0]) | (lengths[sink] == 0), 0, jnp.maximum(slack, 0))
    moved = jax.random.randint(jax.random.fold_in(own, 4), (count // 2,), 0, 1 << 20) % (slack + 1)
    lengths = lengths.at[donor].add(-moved).at[sink].add(moved)
    members = jnp.searchsorted(jnp.cumsum(lengths), jnp.arange(rows * top), side="right").astype(jnp.int32)
    table = members.reshape(top, rows).T
    table = table[jax.random.permutation(jax.random.fold_in(own, 1), rows)]
    offset_by = jax.random.randint(jax.random.fold_in(own, 2), (rows, 1), 0, top)
    return jnp.take_along_axis(table, (jnp.arange(top)[None, :] + offset_by) % top, axis=1)


def load_shares(amount, total, limit, slope, full):
    loads = [(1 << 20) // math.isqrt(grade ** slope) + 1 for grade in range(1, amount + 1)]
    largest = limit if full else min(limit, max(-(-total // amount), total * loads[0] // sum(loads)))
    least = 1 if total - largest >= amount - 1 else 0
    holding, spare = [largest] + [least] * (amount - 1), total - largest - least * (amount - 1)
    while spare > 0:
        movable = [i for i in range(1, amount) if holding[i] < largest] or [i for i in range(1, amount) if holding[i] < limit]
        whole, remaining = sum([loads[i] for i in movable]), spare
        for i in movable:
            extra = min(limit - holding[i], max(1, remaining * loads[i] // whole), spare)
            holding[i] = holding[i] + extra
            spare = spare - extra
    return np.array(holding)


def centred(rng, dims, spread, most, pieces=(), held_as=jnp.bfloat16):
    result = jax.random.normal(rng, dims, jnp.float32) * spread
    if len(pieces) > 0:
        result = block_levels(rng, dims, pieces, -0.22, 0.18) * result
    return jnp.clip(result, min=-most, max=most).astype(held_as)


def setup_inputs(seed: int = 0) -> dict:
    key_of = jax.random.split(jax.random.key(seed), 7)
    entering = centred(key_of[0], (SECTIONS, TOKENS, D), 1.0, 6.0, ((0, 8), (1, 64)))
    saved = centred(key_of[1], (SECTIONS, N_EXPERT, N_EXPERT * CAP, 2 * HDEV), 1.0, 6.0, ((0, 8), (1, 64)))
    routes_keys = jax.random.split(jax.random.fold_in(key_of[2], 1), 2 * SECTIONS * TOKENS // TOK_DEV)
    routes_turns = jax.random.permutation(jax.random.fold_in(key_of[2], 3), 2 * SECTIONS * TOKENS // TOK_DEV)
    routes = jax.vmap(lambda own, number: assign_block(jax.random.fold_in(key_of[2], 2), own, number, TOK_DEV, EXPERTS, TOP, CAP, 2))(routes_keys, routes_turns).reshape((2, SECTIONS, TOKENS, TOP))
    gates = jnp.clip(0.1 + 0.9 * jax.random.uniform(key_of[3], (2, SECTIONS, TOKENS, TOP), jnp.float32) ** block_levels(key_of[3], (2, SECTIONS, TOKENS, TOP), ((1, 8), (2, 64)), -0.2, 0.2), 0.1, 1.0)
    w_in = centred(key_of[4], (SECTIONS, N_EXPERT, D, 2 * HDEV), D ** -0.5, 0.09375, ((0, 8), (1, 64)))
    w_out = centred(key_of[5], (SECTIONS, N_EXPERT, HDEV, D), F ** -0.5, 0.15625, ((0, 8), (1, 64)))
    return {"entering": entering, "saved": saved, "routes": routes, "gates": gates, "w_in": w_in, "w_out": w_out}


def silu_slope(gate_vals):
    sigmoid_vals = jax.nn.sigmoid(gate_vals)
    return sigmoid_vals * (1.0 + gate_vals * (1.0 - sigmoid_vals))


def slot_rows(routes):
    per_block = routes.reshape(N_EXPERT, TOK_DEV * TOP)
    expert_ids = jnp.arange(EXPERTS, dtype=jnp.int32)
    onehot = (per_block[:, :, None] == expert_ids[None, None, :]).astype(jnp.int32)
    before = (jnp.cumsum(onehot, axis=1) - onehot).astype(jnp.int32)
    slot_ids = jnp.sum(before * onehot, axis=2).astype(jnp.int32)
    block_ids = jnp.arange(N_EXPERT, dtype=jnp.int32)[:, None]
    return (block_ids * CAP + slot_ids).astype(jnp.int32).reshape(TOKENS, TOP)


def place_rows(data, routes, rows_at):
    buffer = jnp.zeros((EXPERTS, N_EXPERT * CAP, D), data.dtype)
    source = jnp.broadcast_to(data[:, None, :], (TOKENS, TOP, D))
    return buffer.at[routes, rows_at].set(source)


def expert_forward(packed):
    token_rows, w_in_e, w_out_e = packed
    pre_act = jnp.einsum("rd,jdh->jrh", token_rows.astype(jnp.float32), w_in_e.astype(jnp.float32))
    gate_vals = pre_act[..., :HDEV]
    up_vals = pre_act[..., HDEV:]
    hidden = (jax.nn.silu(gate_vals) * up_vals).astype(jnp.bfloat16)
    slice_part = jnp.einsum("jrh,jhd->jrd", hidden.astype(jnp.float32), w_out_e.astype(jnp.float32)).astype(jnp.bfloat16)
    return jnp.sum(slice_part.astype(jnp.float32), axis=0)


def expert_backward(packed):
    grad_rows, saved_e, w_in_e, w_out_e = packed
    gate_vals = saved_e[..., :HDEV].astype(jnp.float32)
    up_vals = saved_e[..., HDEV:].astype(jnp.float32)
    d_hidden = jnp.einsum("rd,jhd->jrh", grad_rows.astype(jnp.float32), w_out_e.astype(jnp.float32))
    d_gate = d_hidden * up_vals * silu_slope(gate_vals)
    d_up = d_hidden * jax.nn.silu(gate_vals)
    d_pre = jnp.concatenate([d_gate, d_up], axis=-1).astype(jnp.bfloat16)
    slice_back = jnp.einsum("jrh,jdh->jrd", d_pre.astype(jnp.float32), w_in_e.astype(jnp.float32)).astype(jnp.bfloat16)
    return jnp.sum(slice_back.astype(jnp.float32), axis=0)


def combine_rows(inputs, outputs, routes, rows_at, weights):
    picked = outputs[routes, rows_at]
    mixed_sum = jnp.sum(weights[:, :, None] * picked, axis=1)
    return (inputs.astype(jnp.float32) + mixed_sum).astype(jnp.bfloat16)


def forward_map(packed):
    inputs, routes, weights, w_in_s, w_out_s = packed
    rows_at = slot_rows(routes)
    buffer = place_rows(inputs, routes, rows_at)
    w_in_g = w_in_s.reshape(EXPERTS, SHARDS, D, 2 * HDEV)
    w_out_g = w_out_s.reshape(EXPERTS, SHARDS, HDEV, D)
    outputs = lax.map(expert_forward, (buffer, w_in_g, w_out_g))
    return combine_rows(inputs, outputs, routes, rows_at, weights)


def backward_map(packed):
    grad_in, saved_s, routes, weights, w_in_s, w_out_s = packed
    rows_at = slot_rows(routes)
    buffer = place_rows(grad_in, routes, rows_at)
    saved_groups = saved_s.reshape(EXPERTS, SHARDS, N_EXPERT * CAP, 2 * HDEV)
    w_in_g = w_in_s.reshape(EXPERTS, SHARDS, D, 2 * HDEV)
    w_out_g = w_out_s.reshape(EXPERTS, SHARDS, HDEV, D)
    outputs = lax.map(expert_backward, (buffer, saved_groups, w_in_g, w_out_g))
    return combine_rows(grad_in, outputs, routes, rows_at, weights)


def reference(entering, saved, routes, gates, w_in, w_out):
    current = entering
    collected = []
    for tick_idx in range(2):
        fwd_sel = slice(tick_idx % 2, None, 2)
        bwd_sel = slice(1 - tick_idx % 2, None, 2)
        fwd_part = lax.map(forward_map, (current[fwd_sel], routes[tick_idx][fwd_sel], gates[tick_idx][fwd_sel], w_in[fwd_sel], w_out[fwd_sel]))
        bwd_part = lax.map(backward_map, (current[bwd_sel], saved[bwd_sel], routes[tick_idx][bwd_sel], gates[tick_idx][bwd_sel], w_in[bwd_sel], w_out[bwd_sel]))
        layer_result = current.at[fwd_sel].set(fwd_part).at[bwd_sel].set(bwd_part)
        collected.append(layer_result)
        if tick_idx == 0:
            zero_block = jnp.zeros((1, TOKENS, D), jnp.bfloat16)
            from_above = jnp.concatenate([layer_result[1:], zero_block], axis=0)
            from_below = jnp.concatenate([zero_block, layer_result[:-1]], axis=0)
            even_section = (jnp.arange(SECTIONS, dtype=jnp.int32) % 2 == 0)[:, None, None]
            current = jnp.where(even_section, from_above, from_below)
    return jnp.stack(collected)
```

```python
import jax
import jax.numpy as jnp
from jax import lax
from jax.sharding import PartitionSpec as P

SHARDS = 8


def shifted(shard, axis, by):
    devices = lax.axis_size(axis)
    pairs = [(i, i + by) for i in range(devices) if 0 <= i + by < devices]
    return lax.ppermute(shard, axis, pairs)


def silu_slope(gate_vals):
    sigmoid_vals = jax.nn.sigmoid(gate_vals)
    return sigmoid_vals * (1.0 + gate_vals * (1.0 - sigmoid_vals))


def routing_places(routes, experts, capacity):
    tok_count = routes.shape[0]
    flat_routes = routes.reshape(tok_count)
    token_ids = jnp.arange(tok_count, dtype=jnp.int32)
    same = flat_routes[:, None] == flat_routes[None, :]
    earlier = token_ids[None, :] < token_ids[:, None]
    slot_ids = jnp.sum(jnp.where(same & earlier, 1, 0), axis=1).astype(jnp.int32)
    targets = flat_routes * capacity + slot_ids
    slot_range = jnp.arange(experts * capacity, dtype=jnp.int32)
    return (slot_range[:, None] == targets[None, :]).astype(jnp.bfloat16)


def expert_forward(token_rows, w_in_dev, w_out_dev):
    pre_act = jnp.dot(token_rows, w_in_dev, preferred_element_type=jnp.float32)
    half_width = w_out_dev.shape[0]
    gate_vals = pre_act[:, :half_width]
    up_vals = pre_act[:, half_width:]
    hidden = (jax.nn.silu(gate_vals) * up_vals).astype(jnp.bfloat16)
    return jnp.dot(hidden, w_out_dev, preferred_element_type=jnp.float32).astype(jnp.bfloat16)


def expert_backward(grad_rows, saved_pre, w_in_dev, w_out_dev):
    half_width = w_out_dev.shape[0]
    gate_vals = saved_pre[:, :half_width].astype(jnp.float32)
    up_vals = saved_pre[:, half_width:].astype(jnp.float32)
    d_hidden = lax.dot_general(
        grad_rows, w_out_dev, (((1,), (1,)), ((), ())), preferred_element_type=jnp.float32
    )
    d_gate = d_hidden * up_vals * silu_slope(gate_vals)
    d_up = d_hidden * jax.nn.silu(gate_vals)
    d_pre = jnp.concatenate([d_gate, d_up], axis=1).astype(jnp.bfloat16)
    return lax.dot_general(
        d_pre, w_in_dev, (((1,), (1,)), ((), ())), preferred_element_type=jnp.float32
    ).astype(jnp.bfloat16)


def shards(entering, saved, routes, gates, w_in, w_out):
    peer_count = lax.axis_size("expert")
    experts = peer_count // SHARDS
    tok_count = entering.shape[1]
    row_width = entering.shape[2]
    top_count = routes.shape[3]
    capacity = min(
        tok_count, max(2, (3 * tok_count * top_count + 2 * experts - 1) // (2 * experts))
    )
    w_in_dev = w_in[0, 0]
    w_out_dev = w_out[0, 0]
    ring = list(range(0, SHARDS, 2)) + list(range(SHARDS - 1, 0, -2))
    slice_groups = [[e * SHARDS + j for j in ring] for e in range(experts)]
    expert_groups = [[e * SHARDS + j for e in range(experts)] for j in range(SHARDS)]
    saved_dev = saved[0, 0].reshape(experts, SHARDS, capacity, -1)
    saved_dev = jnp.stack([saved_dev[:, j] for j in ring]).reshape(peer_count * capacity, -1)
    section_idx = lax.axis_index("section")
    forward_first = section_idx % 2 == 0
    current = entering[0]
    collected = []

    def run_forward(arrived_rows):
        return expert_forward(arrived_rows, w_in_dev, w_out_dev)

    def run_backward(arrived_rows):
        return expert_backward(arrived_rows, saved_dev, w_in_dev, w_out_dev)

    places = [routing_places(routes[t, 0], experts, capacity) for t in range(2)]
    for tick_idx in range(2):
        doing_forward = forward_first if tick_idx == 0 else jnp.logical_not(forward_first)
        placed = places[tick_idx]
        token_rows = jnp.dot(placed, current, preferred_element_type=jnp.float32).astype(
            jnp.bfloat16
        )
        exchanged = lax.all_to_all(
            token_rows.reshape(experts, capacity, row_width),
            "expert",
            split_axis=0,
            concat_axis=0,
            axis_index_groups=expert_groups,
            tiled=True,
        ).reshape(experts * capacity, row_width)
        arrived = lax.all_gather(
            exchanged, "expert", axis=0, axis_index_groups=slice_groups, tiled=True
        )
        expert_out = lax.cond(doing_forward, run_forward, run_backward, arrived)
        summed = lax.psum_scatter(
            expert_out, "expert", scatter_dimension=0, axis_index_groups=slice_groups, tiled=True
        )
        returned = lax.all_to_all(
            summed.reshape(experts, capacity, row_width),
            "expert",
            split_axis=0,
            concat_axis=0,
            axis_index_groups=expert_groups,
            tiled=True,
        ).reshape(experts * capacity, row_width)
        picked = lax.dot_general(
            placed, returned, (((0,), (0,)), ((), ())), preferred_element_type=jnp.float32
        )
        layer_result = (
            current.astype(jnp.float32) + gates[tick_idx, 0, :, :] * picked
        ).astype(jnp.bfloat16)
        collected.append(layer_result)
        if tick_idx == 0:
            from_below = shifted(layer_result, "section", 1)
            from_above = shifted(layer_result, "section", -1)
            current = jnp.where(forward_first, from_above, from_below)
    return jnp.stack(collected)[:, None]


def solution(mesh):
    return jax.shard_map(
        shards,
        mesh=mesh,
        in_specs=(
            P("section", "expert", None),
            P("section", "expert", None, None),
            P(None, "section", "expert", None),
            P(None, "section", "expert", None),
            P("section", "expert", None, None),
            P("section", "expert", None, None),
        ),
        out_specs=P(None, "section", "expert", None),
        check_vma=False,
    )
```

```python
import jax
import jax.numpy as jnp
from jax import lax
from jax.sharding import PartitionSpec as P

SHARDS = 8
QUAD = 4
MEETS = ((0, 1, 2, 3), (0, 1, 2, 3), (2, 3, 0, 1), (2, 3, 0, 1))


def shifted(shard, axis, by):
    devices = lax.axis_size(axis)
    pairs = [(i, i + by) for i in range(devices) if 0 <= i + by < devices]
    return lax.ppermute(shard, axis, pairs)


def silu_slope(gate_vals):
    sigmoid_vals = jax.nn.sigmoid(gate_vals)
    return sigmoid_vals * (1.0 + gate_vals * (1.0 - sigmoid_vals))


def routing_places(routes, experts, capacity):
    tok_count = routes.shape[0]
    flat_routes = routes.reshape(tok_count)
    token_ids = jnp.arange(tok_count, dtype=jnp.int32)
    same = flat_routes[:, None] == flat_routes[None, :]
    earlier = token_ids[None, :] < token_ids[:, None]
    slot_ids = jnp.sum(jnp.where(same & earlier, 1, 0), axis=1).astype(jnp.int32)
    targets = flat_routes * capacity + slot_ids
    slot_range = jnp.arange(experts * capacity, dtype=jnp.int32)
    return (slot_range[:, None] == targets[None, :]).astype(jnp.bfloat16)


def expert_forward(token_rows, w_in_dev, w_out_dev):
    pre_act = jnp.dot(token_rows, w_in_dev, preferred_element_type=jnp.float32)
    half_width = w_out_dev.shape[0]
    gate_vals = pre_act[:, :half_width]
    up_vals = pre_act[:, half_width:]
    hidden = (jax.nn.silu(gate_vals) * up_vals).astype(jnp.bfloat16)
    return jnp.dot(hidden, w_out_dev, preferred_element_type=jnp.float32).astype(jnp.bfloat16)


def expert_backward(grad_rows, saved_pre, w_in_dev, w_out_dev):
    half_width = w_out_dev.shape[0]
    gate_vals = saved_pre[:, :half_width].astype(jnp.float32)
    up_vals = saved_pre[:, half_width:].astype(jnp.float32)
    d_hidden = lax.dot_general(
        grad_rows, w_out_dev, (((1,), (1,)), ((), ())), preferred_element_type=jnp.float32
    )
    d_gate = d_hidden * up_vals * silu_slope(gate_vals)
    d_up = d_hidden * jax.nn.silu(gate_vals)
    d_pre = jnp.concatenate([d_gate, d_up], axis=1).astype(jnp.bfloat16)
    return lax.dot_general(
        d_pre, w_in_dev, (((1,), (1,)), ((), ())), preferred_element_type=jnp.float32
    ).astype(jnp.bfloat16)


def ring_of(first, size):
    return [first + i for i in [*range(0, size, 2), *range(size - 1, 0, -2)]]


def shards(entering, saved, routes, gates, w_in, w_out):
    peer_count = lax.axis_size("expert")
    experts = peer_count // SHARDS
    quads = peer_count // QUAD
    tok_count = entering.shape[1]
    row_width = entering.shape[2]
    top_count = routes.shape[3]
    capacity = min(
        tok_count, max(2, (3 * tok_count * top_count + 2 * experts - 1) // (2 * experts))
    )
    block_rows = quads * capacity
    w_in_dev = w_in[0, 0]
    w_out_dev = w_out[0, 0]
    device_idx = lax.axis_index("expert")

    meeting = [
        [q * QUAD + MEETS[q % len(MEETS)][i] for q in range(quads)] for i in range(QUAD)
    ]
    group_of = {dev: i for i, group in enumerate(meeting) for dev in group}
    rings = [ring_of(q * QUAD, QUAD) for q in range(quads)]
    ring_pairs = [(ring[p], ring[(p + 1) % QUAD]) for ring in rings for p in range(QUAD)]
    came_from = [[0] * QUAD for _ in range(peer_count)]
    for ring in rings:
        for p in range(QUAD):
            came_from[ring[p]] = [group_of[ring[p - k]] for k in range(QUAD)]

    saved_dev = saved[0, 0].reshape(peer_count, capacity, -1)
    saved_groups = jnp.stack(
        [jnp.concatenate([saved_dev[dev] for dev in group]) for group in meeting]
    )
    order = jnp.asarray(came_from, jnp.int32)[device_idx]
    saved_blocks = jnp.concatenate(
        [lax.dynamic_index_in_dim(saved_groups, order[k], keepdims=False) for k in range(QUAD)]
    )

    section_idx = lax.axis_index("section")
    sections = lax.axis_size("section")
    forward_first = section_idx % 2 == 0
    partners = [(i, i ^ 1) for i in range(sections)]
    current = entering[0]
    collected = []

    def run_forward(arrived_rows):
        return expert_forward(arrived_rows, w_in_dev, w_out_dev)

    def run_backward(arrived_rows):
        return expert_backward(arrived_rows, saved_blocks, w_in_dev, w_out_dev)

    def meet(rows):
        return lax.all_to_all(
            rows.reshape(quads, capacity, row_width),
            "expert",
            split_axis=0,
            concat_axis=0,
            axis_index_groups=meeting,
            tiled=True,
        ).reshape(block_rows, row_width)

    places = []
    for tick_idx in range(2):
        placed = routing_places(routes[tick_idx, 0], experts, capacity)
        placed = placed.reshape(experts, 1, capacity, tok_count)
        placed = jnp.broadcast_to(placed, (experts, SHARDS // QUAD, capacity, tok_count))
        places.append(placed.reshape(block_rows, tok_count))

    for tick_idx in range(2):
        doing_forward = forward_first if tick_idx == 0 else jnp.logical_not(forward_first)
        placed = places[tick_idx]
        token_rows = jnp.dot(placed, current, preferred_element_type=jnp.float32).astype(
            jnp.bfloat16
        )
        blocks = [meet(token_rows)]
        for _ in range(QUAD - 1):
            blocks.append(lax.ppermute(blocks[-1], "expert", ring_pairs))
        expert_out = lax.cond(
            doing_forward, run_forward, run_backward, jnp.concatenate(blocks)
        ).reshape(QUAD, block_rows, row_width)
        total = expert_out[1]
        for step in range(1, QUAD):
            got = lax.ppermute(total, "expert", ring_pairs).astype(jnp.float32)
            own = expert_out[(step + 1) % QUAD].astype(jnp.float32)
            total = (got + own).astype(jnp.bfloat16)
        picked = lax.dot_general(
            placed, meet(total), (((0,), (0,)), ((), ())), preferred_element_type=jnp.float32
        )
        layer_result = (
            current.astype(jnp.float32) + gates[tick_idx, 0, :, :] * picked
        ).astype(jnp.bfloat16)
        collected.append(layer_result)
        if tick_idx == 0:
            current = lax.ppermute(layer_result, "section", partners)
    return jnp.stack(collected)[:, None]


def solution(mesh):
    return jax.shard_map(
        shards,
        mesh=mesh,
        in_specs=(
            P("section", "expert", None),
            P("section", "expert", None, None),
            P(None, "section", "expert", None),
            P(None, "section", "expert", None),
            P("section", "expert", None, None),
            P("section", "expert", None, None),
        ),
        out_specs=P(None, "section", "expert", None),
        check_vma=False,
    )
```

```python
import jax
import jax.numpy as jnp
from jax import lax
from jax.sharding import PartitionSpec as P

SHARDS = 8
QUAD = 8
MEETS = ((0, 1, 2, 3, 4, 5, 6, 7), (7, 6, 5, 4, 3, 2, 1, 0))


def shifted(shard, axis, by):
    devices = lax.axis_size(axis)
    pairs = [(i, i + by) for i in range(devices) if 0 <= i + by < devices]
    return lax.ppermute(shard, axis, pairs)


def silu_slope(gate_vals):
    sigmoid_vals = jax.nn.sigmoid(gate_vals)
    return sigmoid_vals * (1.0 + gate_vals * (1.0 - sigmoid_vals))


def routing_places(routes, experts, capacity):
    tok_count = routes.shape[0]
    flat_routes = routes.reshape(tok_count)
    token_ids = jnp.arange(tok_count, dtype=jnp.int32)
    same = flat_routes[:, None] == flat_routes[None, :]
    earlier = token_ids[None, :] < token_ids[:, None]
    slot_ids = jnp.sum(jnp.where(same & earlier, 1, 0), axis=1).astype(jnp.int32)
    targets = flat_routes * capacity + slot_ids
    slot_range = jnp.arange(experts * capacity, dtype=jnp.int32)
    return (slot_range[:, None] == targets[None, :]).astype(jnp.bfloat16)


def expert_forward(token_rows, w_in_dev, w_out_dev):
    pre_act = jnp.dot(token_rows, w_in_dev, preferred_element_type=jnp.float32)
    half_width = w_out_dev.shape[0]
    gate_vals = pre_act[:, :half_width]
    up_vals = pre_act[:, half_width:]
    hidden = (jax.nn.silu(gate_vals) * up_vals).astype(jnp.bfloat16)
    return jnp.dot(hidden, w_out_dev, preferred_element_type=jnp.float32).astype(jnp.bfloat16)


def expert_backward(grad_rows, saved_pre, w_in_dev, w_out_dev):
    half_width = w_out_dev.shape[0]
    gate_vals = saved_pre[:, :half_width].astype(jnp.float32)
    up_vals = saved_pre[:, half_width:].astype(jnp.float32)
    d_hidden = lax.dot_general(
        grad_rows, w_out_dev, (((1,), (1,)), ((), ())), preferred_element_type=jnp.float32
    )
    d_gate = d_hidden * up_vals * silu_slope(gate_vals)
    d_up = d_hidden * jax.nn.silu(gate_vals)
    d_pre = jnp.concatenate([d_gate, d_up], axis=1).astype(jnp.bfloat16)
    return lax.dot_general(
        d_pre, w_in_dev, (((1,), (1,)), ((), ())), preferred_element_type=jnp.float32
    ).astype(jnp.bfloat16)


def ring_of(first, size):
    return [first + i for i in [*range(0, size, 2), *range(size - 1, 0, -2)]]


def shards(entering, saved, routes, gates, w_in, w_out):
    peer_count = lax.axis_size("expert")
    experts = peer_count // SHARDS
    quads = peer_count // QUAD
    tok_count = entering.shape[1]
    row_width = entering.shape[2]
    top_count = routes.shape[3]
    capacity = min(
        tok_count, max(2, (3 * tok_count * top_count + 2 * experts - 1) // (2 * experts))
    )
    block_rows = quads * capacity
    w_in_dev = w_in[0, 0]
    w_out_dev = w_out[0, 0]
    device_idx = lax.axis_index("expert")

    meeting = [
        [q * QUAD + MEETS[q % len(MEETS)][i] for q in range(quads)] for i in range(QUAD)
    ]
    group_of = {dev: i for i, group in enumerate(meeting) for dev in group}
    rings = [ring_of(q * QUAD, QUAD) for q in range(quads)]
    ring_pairs = [(ring[p], ring[(p + 1) % QUAD]) for ring in rings for p in range(QUAD)]
    came_from = [[0] * QUAD for _ in range(peer_count)]
    for ring in rings:
        for p in range(QUAD):
            came_from[ring[p]] = [group_of[ring[p - k]] for k in range(QUAD)]

    rows_of = [
        [dev * capacity + c for dev in group for c in range(capacity)] for group in meeting
    ]
    wanted = [[row for i in came for row in rows_of[i]] for came in came_from]
    wanted = lax.dynamic_index_in_dim(
        jnp.asarray(wanted, jnp.int32), device_idx, keepdims=False
    )
    row_ids = jnp.arange(peer_count * capacity, dtype=jnp.int32)
    picking = (wanted[:, None] == row_ids[None, :]).astype(jnp.bfloat16)
    saved_blocks = jnp.dot(picking, saved[0, 0], preferred_element_type=jnp.float32)
    saved_blocks = jnp.split(saved_blocks.astype(jnp.bfloat16), QUAD)

    section_idx = lax.axis_index("section")
    sections = lax.axis_size("section")
    forward_first = section_idx % 2 == 0
    partners = [(i, i ^ 1) for i in range(sections)]
    current = entering[0]
    collected = []

    def run_expert(rows, saved_rows, doing_forward):
        return lax.cond(
            doing_forward,
            lambda: expert_forward(rows, w_in_dev, w_out_dev),
            lambda: expert_backward(rows, saved_rows, w_in_dev, w_out_dev),
        )

    def added(left, right):
        return (left.astype(jnp.float32) + right.astype(jnp.float32)).astype(jnp.bfloat16)

    def meet(rows):
        return lax.all_to_all(
            rows.reshape(quads, capacity // 2, 2, row_width),
            "expert",
            split_axis=0,
            concat_axis=0,
            axis_index_groups=meeting,
            tiled=True,
        ).reshape(block_rows, row_width)

    places = []
    for tick_idx in range(2):
        placed = routing_places(routes[tick_idx, 0], experts, capacity)
        placed = placed.reshape(experts, 1, capacity, tok_count)
        placed = jnp.broadcast_to(placed, (experts, SHARDS // QUAD, capacity, tok_count))
        places.append(placed.reshape(block_rows, tok_count))

    for tick_idx in range(2):
        doing_forward = forward_first if tick_idx == 0 else jnp.logical_not(forward_first)
        placed = places[tick_idx]
        token_rows = jnp.dot(placed, current, preferred_element_type=jnp.float32).astype(
            jnp.bfloat16
        )
        block = meet(token_rows)
        own = run_expert(block, saved_blocks[0], doing_forward)
        total = None
        for step in range(1, QUAD):
            block = lax.ppermute(block, "expert", ring_pairs)
            result = run_expert(block, saved_blocks[step], doing_forward)
            total = result if total is None else added(total, result)
            total = lax.ppermute(total, "expert", ring_pairs)
        total = added(total, own)
        picked = lax.dot_general(
            placed, meet(total), (((0,), (0,)), ((), ())), preferred_element_type=jnp.float32
        )
        layer_result = (
            current.astype(jnp.float32) + gates[tick_idx, 0, :, :] * picked
        ).astype(jnp.bfloat16)
        collected.append(layer_result)
        if tick_idx == 0:
            current = lax.ppermute(layer_result, "section", partners)
    return jnp.stack(collected)[:, None]


def solution(mesh):
    return jax.shard_map(
        shards,
        mesh=mesh,
        in_specs=(
            P("section", "expert", None),
            P("section", "expert", None, None),
            P(None, "section", "expert", None),
            P(None, "section", "expert", None),
            P("section", "expert", None, None),
            P("section", "expert", None, None),
        ),
        out_specs=P(None, "section", "expert", None),
        check_vma=False,
    )
```

```python
import jax
import jax.numpy as jnp
from jax import lax
from jax.sharding import PartitionSpec as P

SHARDS = 8
QUAD = 8
MEETS = ((0, 1, 2, 3, 4, 5, 6, 7), (7, 6, 5, 4, 3, 2, 1, 0))


def shifted(shard, axis, by):
    devices = lax.axis_size(axis)
    pairs = [(i, i + by) for i in range(devices) if 0 <= i + by < devices]
    return lax.ppermute(shard, axis, pairs)


def silu_slope(gate_vals):
    sigmoid_vals = jax.nn.sigmoid(gate_vals)
    return sigmoid_vals * (1.0 + gate_vals * (1.0 - sigmoid_vals))


def routing_places(routes, experts, capacity):
    tok_count = routes.shape[0]
    flat_routes = routes.reshape(tok_count)
    token_ids = jnp.arange(tok_count, dtype=jnp.int32)
    same = flat_routes[:, None] == flat_routes[None, :]
    earlier = token_ids[None, :] < token_ids[:, None]
    slot_ids = jnp.sum(jnp.where(same & earlier, 1, 0), axis=1).astype(jnp.int32)
    targets = flat_routes * capacity + slot_ids
    slot_range = jnp.arange(experts * capacity, dtype=jnp.int32)
    return (slot_range[:, None] == targets[None, :]).astype(jnp.bfloat16)


def forward_hidden(token_rows, w_in_dev, half_width):
    pre_act = jnp.dot(token_rows, w_in_dev, preferred_element_type=jnp.float32)
    gate_vals = pre_act[:, :half_width]
    up_vals = pre_act[:, half_width:]
    hidden = (jax.nn.silu(gate_vals) * up_vals).astype(jnp.bfloat16)
    return jnp.concatenate([hidden, jnp.zeros_like(hidden)], axis=1)


def backward_hidden(grad_rows, saved_pre, w_out_dev):
    half_width = w_out_dev.shape[0]
    gate_vals = saved_pre[:, :half_width].astype(jnp.float32)
    up_vals = saved_pre[:, half_width:].astype(jnp.float32)
    d_hidden = lax.dot_general(
        grad_rows, w_out_dev, (((1,), (1,)), ((), ())), preferred_element_type=jnp.float32
    )
    d_gate = d_hidden * up_vals * silu_slope(gate_vals)
    d_up = d_hidden * jax.nn.silu(gate_vals)
    return jnp.concatenate([d_gate, d_up], axis=1).astype(jnp.bfloat16)


def joined(part, total):
    if total is not None:
        part = part + total.astype(jnp.float32)
    return part.astype(jnp.bfloat16)


def forward_out(hidden, total, w_out_dev):
    half_width = w_out_dev.shape[0]
    part = jnp.dot(hidden[:, :half_width], w_out_dev, preferred_element_type=jnp.float32)
    return lax.optimization_barrier(joined(part, total))


def backward_out(d_pre, total, w_in_dev):
    part = lax.dot_general(
        d_pre, w_in_dev, (((1,), (1,)), ((), ())), preferred_element_type=jnp.float32
    )
    return lax.optimization_barrier(joined(part, total))


def ring_of(first, size):
    return [first + i for i in [*range(0, size, 2), *range(size - 1, 0, -2)]]


def shards(entering, saved, routes, gates, w_in, w_out):
    peer_count = lax.axis_size("expert")
    experts = peer_count // SHARDS
    quads = peer_count // QUAD
    tok_count = entering.shape[1]
    row_width = entering.shape[2]
    top_count = routes.shape[3]
    capacity = min(
        tok_count, max(2, (3 * tok_count * top_count + 2 * experts - 1) // (2 * experts))
    )
    block_rows = quads * capacity
    w_in_dev = w_in[0, 0]
    w_out_dev = w_out[0, 0]
    device_idx = lax.axis_index("expert")

    meeting = [
        [q * QUAD + MEETS[q % len(MEETS)][i] for q in range(quads)] for i in range(QUAD)
    ]
    group_of = {dev: i for i, group in enumerate(meeting) for dev in group}
    rings = [ring_of(q * QUAD, QUAD) for q in range(quads)]
    ring_pairs = [(ring[p], ring[(p + 1) % QUAD]) for ring in rings for p in range(QUAD)]
    came_from = [[0] * QUAD for _ in range(peer_count)]
    for ring in rings:
        for p in range(QUAD):
            came_from[ring[p]] = [group_of[ring[p - k]] for k in range(QUAD)]

    rows_of = [
        [dev * capacity + c for dev in group for c in range(capacity)] for group in meeting
    ]
    wanted = [[row for i in came for row in rows_of[i]] for came in came_from]
    wanted = lax.dynamic_index_in_dim(
        jnp.asarray(wanted, jnp.int32), device_idx, keepdims=False
    )
    row_ids = jnp.arange(peer_count * capacity, dtype=jnp.int32)
    picking = (wanted[:, None] == row_ids[None, :]).astype(jnp.bfloat16)
    saved_blocks = jnp.dot(picking, saved[0, 0], preferred_element_type=jnp.float32)
    saved_blocks = jnp.split(saved_blocks.astype(jnp.bfloat16), QUAD)

    section_idx = lax.axis_index("section")
    sections = lax.axis_size("section")
    forward_first = section_idx % 2 == 0
    partners = [(i, i ^ 1) for i in range(sections)]
    current = entering[0]
    collected = []

    def start_expert(rows, saved_rows, doing_forward):
        return lax.cond(
            doing_forward,
            lambda: forward_hidden(rows, w_in_dev, w_out_dev.shape[0]),
            lambda: backward_hidden(rows, saved_rows, w_out_dev),
        )

    def end_expert(hidden, total, doing_forward):
        return lax.cond(
            doing_forward,
            lambda: forward_out(hidden, total, w_out_dev),
            lambda: backward_out(hidden, total, w_in_dev),
        )

    def meet(rows):
        return lax.all_to_all(
            rows.reshape(quads, capacity // 2, 2, row_width),
            "expert",
            split_axis=0,
            concat_axis=0,
            axis_index_groups=meeting,
            tiled=True,
        ).reshape(block_rows, row_width)

    places = []
    for tick_idx in range(2):
        placed = routing_places(routes[tick_idx, 0], experts, capacity)
        placed = placed.reshape(experts, 1, capacity, tok_count)
        placed = jnp.broadcast_to(placed, (experts, SHARDS // QUAD, capacity, tok_count))
        places.append(placed.reshape(block_rows, tok_count))

    for tick_idx in range(2):
        doing_forward = forward_first if tick_idx == 0 else jnp.logical_not(forward_first)
        placed = places[tick_idx]
        token_rows = jnp.dot(placed, current, preferred_element_type=jnp.float32).astype(
            jnp.bfloat16
        )
        block = meet(token_rows)
        own = start_expert(block, saved_blocks[0], doing_forward)
        total = None
        for step in range(1, QUAD):
            block = lax.ppermute(block, "expert", ring_pairs)
            hidden = start_expert(block, saved_blocks[step], doing_forward)
            total = end_expert(hidden, total, doing_forward)
            total = lax.ppermute(total, "expert", ring_pairs)
        total = end_expert(own, total, doing_forward)
        picked = lax.dot_general(
            placed, meet(total), (((0,), (0,)), ((), ())), preferred_element_type=jnp.float32
        )
        layer_result = (
            current.astype(jnp.float32) + gates[tick_idx, 0, :, :] * picked
        ).astype(jnp.bfloat16)
        collected.append(layer_result)
        if tick_idx == 0:
            current = lax.ppermute(layer_result, "section", partners)
    return jnp.stack(collected)[:, None]


def solution(mesh):
    return jax.shard_map(
        shards,
        mesh=mesh,
        in_specs=(
            P("section", "expert", None),
            P("section", "expert", None, None),
            P(None, "section", "expert", None),
            P(None, "section", "expert", None),
            P("section", "expert", None, None),
            P("section", "expert", None, None),
        ),
        out_specs=P(None, "section", "expert", None),
        check_vma=False,
    )
```
